32 devices in a mesh: dp: 8 (over y, x, core), tensor: 4 (over z).
Axes of the slice: x: 2, y: 2, z: 4, core: 2. Of those that a mesh axis runs over, the one named last changes fastest.
Arguments:
- tokens: bfloat16 [8192, 768], P(('dp', 'tensor')), may hold values from -6 to 6
- segments: int32 [8192], P('dp'), may hold values from 0 to 3, as said below
- buckets: int32 [1024], replicated, may hold values from 0 to 31, as said below
- routes: int32 [8192, 2], P(('dp', 'tensor')), may hold values from 0 to 7, all different within a row; in each aligned block of 256 rows (0 to 255, 256 to 511, ...) at most 128 rows name the same one
- norm_one: float32 [768], replicated, may hold values from 0.5 to 1.5
- w_qkv: bfloat16 [768, 3, 768], P(None, None, 'tensor'), may hold values from -0.21875 to 0.21875
- w_out: bfloat16 [768, 768], P('tensor'), may hold values from -0.625 to 0.625
- rel_bias: float32 [32, 12], P(None, 'tensor'), may hold values from -4 to 4
- norm_two: float32 [768], replicated, may hold values from 0.5 to 1.5
- w_router: bfloat16 [768, 8], replicated, may hold values from -0.21875 to 0.21875
- w_gate: bfloat16 [8, 768, 3072], P('dp', None, 'tensor'), may hold values from -0.21875 to 0.21875
- w_up: bfloat16 [8, 768, 3072], P('dp', None, 'tensor'), may hold values from -0.21875 to 0.21875
- w_down: bfloat16 [8, 3072, 768], P('dp', 'tensor'), may hold values from -0.875 to 0.875
- cotangent: bfloat16 [8192, 768], P(('dp', 'tensor')), may hold values from -6 to 6
Outputs:
- mixed_out: bfloat16 [8192, 768], P(('dp', 'tensor'))
- grad_tokens: bfloat16 [8192, 768], P(('dp', 'tensor'))
- grad_norm_one: float32 [768], replicated
- grad_qkv: float32 [768, 3, 768], P(None, None, 'tensor')
- grad_out: float32 [768, 768], P('tensor')
- grad_bias: float32 [32, 12], P(None, 'tensor')
- grad_norm_two: float32 [768], replicated
- grad_router: float32 [768, 8], replicated
- grad_gate: float32 [8, 768, 3072], P('dp', None, 'tensor')
- grad_up: float32 [8, 768, 3072], P('dp', None, 'tensor')
- grad_down: float32 [8, 3072, 768], P('dp', 'tensor')
The draws below stay inside these ranges and needn't reach their ends.
Inputs may be any that keep to these rules, and one draw needn't show every extreme that they name: `segments`: within each block of 1024 slots of one index of dp the ids start at 0, never fall and rise by one from a sequence to the next; a sequence is a run of equal ids; in every draw some block holds a single sequence of 1024 tokens and some block four sequences. `buckets`: starts at 0, never falls, rises by at most one from a distance to the next, and ends at 31. `routes`: each row names 2 different experts; in each aligned block of 256 rows (the rows of one device) no expert is named by more than 128 rows, a bound that some block reaches.
All inputs are finite; a program needn't handle non-finite values.
Results may differ from the reference program's by a relative error of at most 0.025.
Values may be sent and summed in bfloat16 or wider, within the bound.
A program may use at most 192 MiB of HBM per device.

```python
import math
import jax
import jax.numpy as jnp
import numpy as np
from jax import lax

D = 768
HEADS = 12
HD = 64
FF = 3072
EXPERTS = 8
TOPK = 2
NB = 32
TOK_DEV = 1024
TOKENS = 8192
ROWS_DEV = 256
CAP_Q = 128
ROWS_EXP = 4096
FF_DEV = 768
N_DP = 8
N_TENSOR = 4


def draw_segments(key, part):
    keys = jax.random.split(jax.random.fold_in(key, 11), 4)
    third = TOK_DEV // 3
    offsets = jnp.arange(3, dtype=jnp.int32) * third
    starts = offsets[None, :] + jax.random.randint(keys[0], (N_DP, 3), 1, third + 1)
    counts = jax.random.randint(keys[1], (N_DP,), 0, 4)
    single = jax.random.randint(keys[2], (), 0, N_DP)
    busiest = (single + 1 + jax.random.randint(keys[3], (), 0, N_DP - 1)) % N_DP
    blocks = jnp.arange(N_DP, dtype=jnp.int32)
    counts = jnp.where(blocks == single, 0, counts)
    counts = jnp.where(blocks == busiest, 3, counts)
    positions = jnp.arange(TOK_DEV, dtype=jnp.int32)
    order = jnp.arange(3, dtype=jnp.int32)
    passed = (positions[None, None, :] >= starts[:, :, None]) & (order[None, :, None] < counts[:, None, None])
    ids = jnp.sum(passed.astype(jnp.int32), axis=1)
    return ids.reshape(-1).astype(jnp.int32)


def draw_buckets(key, part):
    half = NB // 2
    chosen = jax.random.permutation(jax.random.fold_in(key, 23), TOK_DEV - half - 1)[:half - 1] + half + 1
    distance = jnp.arange(TOK_DEV, dtype=jnp.int32)
    rises = jnp.sum((distance[:, None] >= chosen[None, :]).astype(jnp.int32), axis=1)
    return (jnp.minimum(distance, half) + rises).astype(jnp.int32)


def steps_of(key, extent, cuts, least, top_value):
    level = 1.0
    for position, shards_of in cuts:
        draws = jax.random.uniform(jax.random.fold_in(jax.random.fold_in(key, 6), position), (shards_of,), jnp.float32, least / len(cuts), top_value / len(cuts))
        level = level * jnp.repeat(jnp.exp(draws), extent[position] // shards_of).reshape((-1,) + (1,) * (len(extent) - 1 - position))
    return level


def shared_out(stream_key, own, number, rows, number_of, top, limit, slope):
    sequence = jax.random.permutation(stream_key, number_of)
    heavy_load, common = load_shares(number_of, rows * top, limit, slope, True), load_shares(number_of, rows * top, limit, slope, False)
    places = jnp.arange(number_of)

    def named(lengths, turn):
        used = int((lengths > 0).sum())
        fixed = max(1, used // 4)
        moved = fixed + (places - fixed + turn * (used - fixed)) % max(1, number_of - fixed)
        return jnp.zeros((number_of,), jnp.int32).at[sequence[jnp.where(places < fixed, places, moved)]].set(jnp.asarray(lengths, jnp.int32))

    lengths = jnp.where(number % 4 == 0, named(heavy_load, number // 4), named(common, number - number // 4 - 1))
    mixed = jax.random.permutation(jax.random.fold_in(own, 3), number_of)
    donor, taker = mixed[0:number_of // 2 * 2:2], mixed[1:number_of // 2 * 2:2]
    room = jnp.minimum(lengths[donor] - 1, limit - lengths[taker]) // 2
    room = jnp.where((donor == sequence[0]) | (taker == sequence[0]) | (lengths[taker] == 0), 0, jnp.maximum(room, 0))
    moved = jax.random.randint(jax.random.fold_in(own, 4), (number_of // 2,), 0, 1 << 20) % (room + 1)
    lengths = lengths.at[donor].add(-moved).at[taker].add(moved)
    labels = jnp.searchsorted(jnp.cumsum(lengths), jnp.arange(rows * top), side="right").astype(jnp.int32)
    grid = labels.reshape(top, rows).T
    grid = grid[jax.random.permutation(jax.random.fold_in(own, 1), rows)]
    turn = jax.random.randint(jax.random.fold_in(own, 2), (rows, 1), 0, top)
    return jnp.take_along_axis(grid, (jnp.arange(top)[None, :] + turn) % top, axis=1)


def load_shares(number_of, total, reach, skew, full):
    portions = [(1 << 20) // math.isqrt(grade ** skew) + 1 for grade in range(1, number_of + 1)]
    largest = reach if full else min(reach, max(-(-total // number_of), total * portions[0] // sum(portions)))
    least = 1 if total - largest >= number_of - 1 else 0
    given, rest = [largest] + [least] * (number_of - 1), total - largest - least * (number_of - 1)
    while rest > 0:
        free = [i for i in range(1, number_of) if given[i] < largest] or [i for i in range(1, number_of) if given[i] < reach]
        pool, remaining = sum([portions[i] for i in free]), rest
        for i in free:
            more = min(reach - given[i], max(1, remaining * portions[i] // pool), rest)
            given[i] = given[i] + more
            rest = rest - more
    return np.array(given)


def bell_draw(rng, dims, deviation, limit, shards=(), kind=jnp.bfloat16):
    drawn = deviation * jax.random.normal(rng, dims, jnp.float32)
    if shards:
        drawn = drawn * steps_of(rng, dims, shards, -0.22, 0.18)
    return jnp.clip(drawn, -limit, limit).astype(kind)


def setup_inputs(seed: int = 0) -> dict:
    arg_keys = jax.random.split(jax.random.key(seed), 15)
    tokens = bell_draw(arg_keys[0], (TOKENS, D), 1.0, 6.0, ((0, 32),))
    segments = draw_segments(jax.random.fold_in(arg_keys[14], 71), 0)
    buckets = draw_buckets(jax.random.fold_in(arg_keys[14], 71), 0)
    routes_keys = jax.random.split(jax.random.fold_in(arg_keys[3], 1), TOKENS // ROWS_DEV)
    routes_turns = jax.random.permutation(jax.random.fold_in(arg_keys[3], 3), TOKENS // ROWS_DEV)
    routes = jax.vmap(lambda own, number: shared_out(jax.random.fold_in(arg_keys[3], 2), own, number, ROWS_DEV, EXPERTS, TOPK, CAP_Q, 1))(routes_keys, routes_turns).reshape((TOKENS, TOPK))
    norm_one = jnp.clip(1.0 + 0.1 * jax.random.normal(arg_keys[4], (D,), jnp.float32), 0.5, 1.5)
    w_qkv = bell_draw(arg_keys[5], (D, 3, HEADS * HD), D ** -0.5, 0.21875, ((2, 4),))
    w_out = bell_draw(arg_keys[6], (HEADS * HD, D), (HEADS * HD // 8) ** -0.5, 0.625, ((0, 4),))
    rel_bias = bell_draw(arg_keys[7], (NB, HEADS), 1.0, 4.0, ((1, 4),), jnp.float32)
    norm_two = jnp.clip(1.0 + 0.1 * jax.random.normal(arg_keys[8], (D,), jnp.float32), 0.5, 1.5)
    w_router = bell_draw(arg_keys[9], (D, EXPERTS), D ** -0.5, 0.21875)
    w_gate = bell_draw(arg_keys[10], (EXPERTS, D, FF), D ** -0.5, 0.21875, ((0, 8), (2, 4)))
    w_up = bell_draw(arg_keys[11], (EXPERTS, D, FF), D ** -0.5, 0.21875, ((0, 8), (2, 4)))
    w_down = bell_draw(arg_keys[12], (EXPERTS, FF, D), (max(1, FF // (EXPERTS * EXPERTS))) ** -0.5, 0.875, ((0, 8), (1, 4)))
    cotangent = bell_draw(arg_keys[13], (TOKENS, D), 1.0, 6.0, ((0, 32),))
    return dict(tokens=tokens, segments=segments, buckets=buckets, routes=routes, norm_one=norm_one, w_qkv=w_qkv, w_out=w_out, rel_bias=rel_bias, norm_two=norm_two, w_router=w_router, w_gate=w_gate, w_up=w_up, w_down=w_down, cotangent=cotangent)


@jax.custom_vjp
def low(v):
    return lax.optimization_barrier(v.astype(jnp.bfloat16)).astype(jnp.float32)

@jax.custom_vjp
def low_back(v):
    return v

def low_keep(v):
    return (low(v), None)

def low_pass(kept, grad):
    return (grad,)

def back_keep(v):
    return (v, None)

def back_low(kept, grad):
    return (low(grad),)
low.defvjp(low_keep, low_pass)
low_back.defvjp(back_keep, back_low)
EPSILON = 1e-06
HIGHEST = lax.Precision.HIGHEST

def rms_scale(values, gain):
    inverse = lax.rsqrt(lax.optimization_barrier(jnp.mean(values * values, axis=-1, keepdims=True)) + EPSILON)
    return values * inverse * gain

def attend_block(query, key, value, segment, bias_dist):
    scale = HD ** (-0.5)
    positions = jnp.arange(TOK_DEV, dtype=jnp.int32)
    distance = positions[:, None] - positions[None, :]
    allowed = (distance >= 0) & (segment[:, None] == segment[None, :])
    bias = jnp.take(bias_dist, jnp.maximum(distance, 0), axis=1)
    scores = jnp.einsum('ihd,jhd->hij', query, key, precision=HIGHEST) * scale + bias
    scores = low_back(scores)
    masked = jnp.where(allowed[None], scores, -1e+30)
    peak = lax.optimization_barrier(jnp.max(masked, axis=2, keepdims=True))
    weights = jnp.exp(masked - peak)
    probs = weights / lax.optimization_barrier(jnp.sum(weights, axis=2, keepdims=True))
    probs_low = low(probs)
    context = jnp.einsum('hij,jhd->ihd', probs_low, value, precision=HIGHEST)
    return low_back(low(context)).reshape(TOK_DEV, HEADS * HD)

def expert_rows(block):
    rows, gate_weight, up_weight, down_weight = block
    total = jnp.zeros((ROWS_EXP, D), jnp.float32)
    for group in range(N_TENSOR):
        lower = group * FF_DEV
        upper = lower + FF_DEV
        inputs = low_back(rows)
        pre_gate = low_back(jnp.dot(inputs, gate_weight[:, lower:upper], precision=HIGHEST))
        pre_up = low_back(jnp.dot(inputs, up_weight[:, lower:upper], precision=HIGHEST))
        active = low(jax.nn.gelu(pre_gate, approximate=True) * pre_up)
        total = total + low(jnp.dot(active, down_weight[lower:upper, :], precision=HIGHEST))
    return total

def prepare(routes):
    expert_ids = routes.reshape(N_DP * N_TENSOR, ROWS_DEV * TOPK)
    member = (expert_ids[:, :, None] == jnp.arange(EXPERTS, dtype=jnp.int32)[None, None, :]).astype(jnp.int32)
    earlier = jnp.cumsum(member, axis=1) - member
    place = lax.optimization_barrier(jnp.sum(earlier * member, axis=2))
    device = jnp.arange(N_DP * N_TENSOR, dtype=jnp.int32)[:, None]
    row_in = (device * CAP_Q + place).reshape(-1).astype(jnp.int32)
    expert_flat = expert_ids.reshape(-1)
    owner = jnp.full((EXPERTS, ROWS_EXP), -1, dtype=jnp.int32).at[expert_flat, row_in].set(jnp.arange(TOKENS * TOPK, dtype=jnp.int32))
    return (expert_flat, row_in, owner)

def reference(tokens, segments, buckets, routes, norm_one, w_qkv, w_out, rel_bias, norm_two, w_router, w_gate, w_up, w_down, cotangent):
    expert_flat, row_in, owner = prepare(routes)
    filled = owner >= 0
    source = jnp.maximum(owner, 0) // TOPK
    choose = (routes[:, :, None] == jnp.arange(EXPERTS, dtype=jnp.int32)[None, None, :]).astype(jnp.float32)
    segment_blocks = segments.reshape(N_DP, TOK_DEV)

    def forward(inputs, gain_one, qkv_weight, out_weight, bias_table, gain_two, router_weight, gate_weight, up_weight, down_weight):
        normed_one = low(rms_scale(inputs, gain_one))
        projected = jnp.dot(normed_one, qkv_weight.reshape(D, 3 * HEADS * HD), precision=HIGHEST)
        projected = low_back(low(projected))
        parts = projected.reshape(N_DP, TOK_DEV, 3, HEADS, HD)
        bias_dist = bias_table[buckets, :].T

        def one_block(block):
            return attend_block(block[0], block[1], block[2], block[3], bias_dist)
        context = lax.map(jax.checkpoint(one_block), (parts[:, :, 0], parts[:, :, 1], parts[:, :, 2], segment_blocks))
        context = context.reshape(TOKENS, HEADS * HD)
        attended = low_back(jnp.dot(context, out_weight, precision=HIGHEST))
        hidden = inputs + attended
        normed_two = low(rms_scale(hidden, gain_two))
        logits = low_back(jnp.dot(normed_two, router_weight, precision=HIGHEST))
        router = jax.nn.softmax(logits, axis=-1)
        gate_vals = lax.optimization_barrier(jnp.sum(choose * router[:, None, :], axis=2))
        gathered = jnp.where(filled[:, :, None], normed_two[source], 0.0)
        outputs = lax.map(jax.checkpoint(expert_rows), (gathered, gate_weight, up_weight, down_weight))
        pair_out = low_back(outputs[expert_flat, row_in].reshape(TOKENS, TOPK, D))
        return hidden + lax.optimization_barrier(jnp.sum(gate_vals[:, :, None] * pair_out, axis=1))
    mixed, pullback = jax.vjp(forward, tokens.astype(jnp.float32), norm_one, w_qkv.astype(jnp.float32), w_out.astype(jnp.float32), rel_bias, norm_two, w_router.astype(jnp.float32), w_gate.astype(jnp.float32), w_up.astype(jnp.float32), w_down.astype(jnp.float32))
    grads = pullback(cotangent.astype(jnp.float32))
    return (mixed.astype(jnp.bfloat16), grads[0].astype(jnp.bfloat16), grads[1], grads[2], grads[3], grads[4], grads[5], grads[6], grads[7], grads[8], grads[9])
```

```python
import functools

import jax
import jax.numpy as jnp
from jax import lax
from jax.experimental import pallas as pl
from jax.experimental.pallas import tpu as pltpu
from jax.sharding import PartitionSpec as P

HD = 64


EPSILON = 1e-06
HIGHEST = lax.Precision.HIGHEST


def contract(left, right, left_dim, right_dim):
    return lax.dot_general(
        left, right, (((left_dim,), (right_dim,)), ((), ())), preferred_element_type=jnp.float32
    )


def gated(pre_gate, pre_up):
    return jax.nn.gelu(pre_gate, approximate=True) * pre_up


def exchange(rows):
    return lax.all_to_all(rows, "dp", split_axis=0, concat_axis=0, tiled=True)


def total_over_all(part):
    count = lax.axis_size("dp") * lax.axis_size("tensor")
    if count > 64:
        return lax.psum(part, ("dp", "tensor"))
    return jnp.sum(lax.all_gather(part, ("dp", "tensor"), axis=0), axis=0)


def turned(table, first, width):
    return jnp.concatenate(
        [table[:, : first + 1][:, ::-1], table[:, first + 1 : width][:, ::-1]], axis=1
    )


def dot(left, right, left_dim, right_dim):
    return lax.dot_general(
        left, right, (((left_dim,), (right_dim,)), ((), ())), preferred_element_type=jnp.float32
    )


def block_probs(proj_ref, seg_col_ref, seg_row_ref, bias_ref, head, heads, first, block, scale):
    width = first + block
    inner = heads * HD
    rows = slice(first, width)
    query = proj_ref[rows, head * HD : (head + 1) * HD]
    key = proj_ref[:width, inner + head * HD : inner + (head + 1) * HD]
    base = jnp.broadcast_to(bias_ref[head, first // block, :width][None, :], (block, width))
    bias = pltpu.roll(base, 0, 1, stride=1, stride_axis=0)
    row = lax.broadcasted_iota(jnp.int32, (block, width), 0) + first
    column = lax.broadcasted_iota(jnp.int32, (block, width), 1)
    allowed = (column <= row) & (seg_col_ref[rows, :] == seg_row_ref[:, :width])
    scores = jnp.where(allowed, dot(query, key, 1, 1) * scale + bias, -1e30)
    weights = jnp.exp(scores - jnp.max(scores, axis=1, keepdims=True))
    return query, key, weights / jnp.sum(weights, axis=1, keepdims=True)


def attend_kernel(heads, block, scale, proj_ref, seg_col_ref, seg_row_ref, bias_ref, context_ref):
    length = proj_ref.shape[0]
    inner = heads * HD
    for first in range(0, length, block):
        width = first + block
        parts = []
        for head in range(heads):
            query, key, probs = block_probs(
                proj_ref, seg_col_ref, seg_row_ref, bias_ref, head, heads, first, block, scale
            )
            value = proj_ref[:width, 2 * inner + head * HD : 2 * inner + (head + 1) * HD]
            parts.append(dot(probs.astype(jnp.bfloat16), value, 1, 0))
        context_ref[first:width, :] = jnp.concatenate(parts, axis=1).astype(jnp.bfloat16)


def attend_back_kernel(
    heads,
    block,
    scale,
    proj_ref,
    grad_ref,
    seg_col_ref,
    seg_row_ref,
    bias_ref,
    rows_ref,
    diag_ref,
    total_ref,
):
    length = proj_ref.shape[0]
    inner = heads * HD
    total_ref[...] = jnp.zeros_like(total_ref)
    diag_ref[...] = jnp.zeros_like(diag_ref)
    flip = (
        lax.broadcasted_iota(jnp.int32, (block, block), 0)
        + lax.broadcasted_iota(jnp.int32, (block, block), 1)
        == block - 1
    ).astype(jnp.bfloat16)
    for first in range(0, length, block):
        width = first + block
        query_parts = []
        for head in range(heads):
            query, key, probs = block_probs(
                proj_ref, seg_col_ref, seg_row_ref, bias_ref, head, heads, first, block, scale
            )
            value = proj_ref[:width, 2 * inner + head * HD : 2 * inner + (head + 1) * HD]
            grad = grad_ref[first:width, head * HD : (head + 1) * HD]
            grad_probs = dot(grad, value, 1, 1)
            row_delta = jnp.sum(probs * grad_probs, axis=1, keepdims=True)
            grad_scores = (probs * (grad_probs - row_delta)).astype(jnp.bfloat16)
            query_parts.append(dot(grad_scores, key, 1, 0) * scale)
            total_ref[0, head, :width, :] += dot(grad_scores, query, 0, 0) * scale
            total_ref[1, head, :width, :] += dot(probs.astype(jnp.bfloat16), grad, 0, 0)
            flipped = dot(flip, grad_scores, 1, 0)
            lined = pltpu.roll(flipped, 0, 1, stride=1, stride_axis=0)
            diag_ref[head, first // block, :width] = jnp.sum(lined, axis=0)
        rows_ref[first:width, :inner] = jnp.concatenate(query_parts, axis=1).astype(jnp.bfloat16)
    for part in range(2):
        rows_ref[:, (1 + part) * inner : (2 + part) * inner] = jnp.concatenate(
            [total_ref[part, head] for head in range(heads)], axis=1
        ).astype(jnp.bfloat16)


def local(
    tokens,
    segments,
    buckets,
    routes,
    norm_one,
    w_qkv,
    w_out,
    rel_bias,
    norm_two,
    w_router,
    w_gate,
    w_up,
    w_down,
    cotangent,
):
    rows_dev = tokens.shape[0]
    width = tokens.shape[1]
    tok_dev = segments.shape[0]
    bucket_count = rel_bias.shape[0]
    heads_local = rel_bias.shape[1]
    inner = heads_local * HD
    experts = w_router.shape[1]
    groups = lax.axis_size("tensor")
    dp_count = lax.axis_size("dp")
    capacity = 4 * tok_dev // (groups * experts)
    top = routes.shape[1]
    block = min(256, tok_dev)
    blocks = tok_dev // block
    scale = HD ** (-0.5)
    upstream = cotangent.astype(jnp.float32)
    values = tokens.astype(jnp.float32)
    inverse_one = lax.rsqrt(jnp.mean(values * values, axis=1, keepdims=True) + EPSILON)
    scaled_one = values * inverse_one
    normed_one = (scaled_one * norm_one).astype(jnp.bfloat16)
    normed_all = lax.all_gather(normed_one, "tensor", axis=0, tiled=True)
    side = jnp.concatenate(
        [
            cotangent,
            jnp.pad(routes.astype(jnp.bfloat16), ((0, 0), (0, 128 - top))),
        ],
        axis=1,
    )
    side_all = lax.all_gather(side, "tensor", axis=0, tiled=True)
    cotangent_all = side_all[:, :width].reshape(groups, rows_dev, width)
    routes_all = side_all[:, width : width + top].astype(jnp.int32).reshape(groups, rows_dev, top)
    choose = (routes_all[..., None] == jnp.arange(experts, dtype=jnp.int32)).astype(jnp.float32)
    member = jnp.sum(choose, axis=2)
    earlier = jnp.tril(jnp.ones((rows_dev, rows_dev), jnp.bfloat16), -1)
    place = jnp.einsum(
        "nm,tme->tne", earlier, member.astype(jnp.bfloat16), preferred_element_type=jnp.float32
    )
    seat = place + capacity * jnp.arange(experts, dtype=jnp.float32)
    slot = jnp.sum(choose * seat[:, :, None, :], axis=3).astype(jnp.int32)
    seats = jnp.arange(experts * capacity, dtype=jnp.int32)
    pick = [slot[:, :, k, None] == seats for k in range(top)]
    pick_any = pick[0]
    for one in pick[1:]:
        pick_any = pick_any | one
    pick_any = pick_any.astype(jnp.bfloat16)

    def send(group_rows):
        seated = jnp.einsum(
            "tnz,tnd->tzd", pick_any, group_rows, preferred_element_type=jnp.float32
        ).astype(jnp.bfloat16)
        ordered = seated.reshape(groups, experts, capacity, width).transpose(1, 0, 2, 3)
        return exchange(ordered.reshape(experts, groups * capacity, width)).reshape(-1, width)

    def fetch(rows_back):
        returned = exchange(rows_back.reshape(dp_count, groups * capacity, width))
        ordered = returned.reshape(experts, groups, capacity, width).transpose(1, 0, 2, 3)
        return ordered.reshape(groups, experts * capacity, width)

    cot_rows = send(cotangent_all)
    proj_weight = w_qkv.reshape(width, 3 * inner)
    projected = jnp.dot(normed_all, proj_weight, preferred_element_type=jnp.float32).astype(
        jnp.bfloat16
    )
    bucket_hot = (buckets[:, None] == jnp.arange(bucket_count, dtype=jnp.int32)[None, :]).astype(
        jnp.float32
    )
    bias_dist = jnp.dot(bucket_hot, rel_bias, precision=HIGHEST).T
    bias_table = jnp.stack(
        [
            jnp.pad(
                turned(bias_dist, first, first + block), ((0, 0), (0, tok_dev - first - block))
            )
            for first in range(0, tok_dev, block)
        ],
        axis=1,
    )
    seg_col = segments[:, None]
    seg_row = segments[None, :]
    flops = 2 * heads_local * tok_dev * tok_dev * HD
    context = pl.pallas_call(
        functools.partial(attend_kernel, heads_local, block, scale),
        out_shape=jax.ShapeDtypeStruct((tok_dev, inner), jnp.bfloat16),
        cost_estimate=pl.CostEstimate(
            flops=2 * flops, bytes_accessed=2 * tok_dev * inner * 4, transcendentals=flops // 128
        ),
    )(projected, seg_col, seg_row, bias_table)
    rows = context
    attended = lax.psum_scatter(
        jnp.dot(rows, w_out, preferred_element_type=jnp.float32).astype(jnp.bfloat16),
        "tensor",
        scatter_dimension=0,
        tiled=True,
    ).astype(jnp.float32)
    hidden = values + attended
    inverse_two = lax.rsqrt(jnp.mean(hidden * hidden, axis=1, keepdims=True) + EPSILON)
    scaled_two = hidden * inverse_two
    normed_two = (scaled_two * norm_two).astype(jnp.bfloat16)
    normed_two_all = lax.all_gather(normed_two, "tensor", axis=0, tiled=True)
    logits = jnp.dot(normed_two_all, w_router, preferred_element_type=jnp.float32)
    router = jax.nn.softmax(logits, axis=1).reshape(groups, rows_dev, experts)
    gate_vals = jnp.sum(choose * router[:, :, None, :], axis=3)
    rows_in = send(normed_two_all.reshape(groups, rows_dev, width))
    own_expert = jnp.arange(experts, dtype=jnp.int32) == lax.axis_index("dp")
    gate_rows = jnp.sum(
        jnp.where(
            own_expert,
            jax.nn.softmax(jnp.dot(rows_in, w_router, preferred_element_type=jnp.float32), axis=1),
            0.0,
        ),
        axis=1,
        keepdims=True,
    )
    grad_in = (gate_rows * cot_rows.astype(jnp.float32)).astype(jnp.bfloat16)
    gate_weight = w_gate[0]
    up_weight = w_up[0]
    down_weight = w_down[0]
    pre_gate = jnp.dot(rows_in, gate_weight, preferred_element_type=jnp.float32)
    pre_up = jnp.dot(rows_in, up_weight, preferred_element_type=jnp.float32)
    active = gated(pre_gate, pre_up).astype(jnp.bfloat16)
    partial_rows = jnp.dot(active, down_weight, preferred_element_type=jnp.float32).astype(
        jnp.bfloat16
    )
    back_rows = fetch(partial_rows)
    upstream_all = cotangent_all.astype(jnp.float32)
    mixing = jnp.zeros((groups, rows_dev, width), jnp.float32)
    grad_gates = []
    for k in range(top):
        pair_out = jnp.einsum(
            "tnz,tzd->tnd",
            pick[k].astype(jnp.bfloat16),
            back_rows,
            preferred_element_type=jnp.float32,
        )
        mixing = mixing + gate_vals[:, :, k, None] * pair_out
        grad_gates.append(jnp.sum(upstream_all * pair_out, axis=2))
    mixed = hidden + lax.psum_scatter(
        mixing.astype(jnp.bfloat16).reshape(tok_dev, width),
        "tensor",
        scatter_dimension=0,
        tiled=True,
    ).astype(jnp.float32)
    grad_gates = jnp.stack(grad_gates, axis=2)
    grad_active = contract(grad_in, down_weight, 1, 1)
    grad_down = contract(active, grad_in, 0, 0)
    unused, pull = jax.vjp(gated, pre_gate, pre_up)
    grad_pre_gate, grad_pre_up = pull(grad_active)
    grad_pre_gate = grad_pre_gate.astype(jnp.bfloat16)
    grad_pre_up = grad_pre_up.astype(jnp.bfloat16)
    grad_gate = contract(rows_in, grad_pre_gate, 0, 0)
    grad_up = contract(rows_in, grad_pre_up, 0, 0)
    grad_rows_x = (
        contract(grad_pre_gate, gate_weight, 1, 1) + contract(grad_pre_up, up_weight, 1, 1)
    ).astype(jnp.bfloat16)
    grad_router_probs = jnp.sum(choose * grad_gates[..., None], axis=2)
    grad_logits = (
        (router * (grad_router_probs - jnp.sum(router * grad_router_probs, axis=2, keepdims=True)))
        .astype(jnp.bfloat16)
        .reshape(tok_dev, experts)
    )
    grad_router = contract(grad_logits, normed_two_all, 0, 0)
    grad_seated = jnp.einsum(
        "tnz,tzd->tnd", pick_any, fetch(grad_rows_x), preferred_element_type=jnp.float32
    ).reshape(tok_dev, width)
    grad_normed_two = lax.psum_scatter(
        (grad_seated + contract(grad_logits, w_router, 1, 1)).astype(jnp.bfloat16),
        "tensor",
        scatter_dimension=0,
        tiled=True,
    ).astype(jnp.float32)
    grad_norm_two = jnp.sum(grad_normed_two * scaled_two, axis=0)
    spread_two = grad_normed_two * norm_two
    grad_hidden = upstream + inverse_two * (
        spread_two - scaled_two * jnp.mean(spread_two * scaled_two, axis=1, keepdims=True)
    )
    grad_attended = grad_hidden.astype(jnp.bfloat16)
    piece = lax.all_gather(grad_attended, "tensor", axis=0, tiled=True)
    rows = context
    grad_out_sum = contract(rows, piece, 0, 0)
    grad_piece = contract(piece, w_out, 1, 1)
    grad_context_all = grad_piece
    grad_out_local, grad_context_all = (grad_out_sum, grad_context_all)
    grad_context = grad_context_all.astype(jnp.bfloat16)
    grad_proj_rows, diagonals = pl.pallas_call(
        functools.partial(attend_back_kernel, heads_local, block, scale),
        out_shape=(
            jax.ShapeDtypeStruct((tok_dev, 3 * inner), jnp.bfloat16),
            jax.ShapeDtypeStruct((heads_local, blocks, tok_dev), jnp.float32),
        ),
        scratch_shapes=[pltpu.VMEM((2, heads_local, tok_dev, HD), jnp.float32)],
        cost_estimate=pl.CostEstimate(
            flops=5 * flops, bytes_accessed=4 * tok_dev * inner * 4, transcendentals=flops // 128
        ),
    )(projected, grad_context, seg_col, seg_row, bias_table)
    by_distance = jnp.zeros((heads_local, tok_dev), jnp.float32)
    for index in range(blocks):
        first = index * block
        reach = first + block
        sums = jnp.roll(diagonals[:, index, :reach], 1 - block, axis=1)
        by_distance = by_distance + jnp.pad(
            turned(sums, first, reach), ((0, 0), (0, tok_dev - reach))
        )
    grad_bias_local = jnp.einsum("hn,nb->bh", by_distance, bucket_hot, precision=HIGHEST)
    grad_qkv_local = contract(normed_all, grad_proj_rows, 0, 0).reshape(width, 3, inner)
    rows = grad_proj_rows
    grad_normed_one = lax.psum_scatter(
        contract(rows, proj_weight, 1, 1).astype(jnp.bfloat16),
        "tensor",
        scatter_dimension=0,
        tiled=True,
    ).astype(jnp.float32)
    grad_norm_one = (
        jnp.sum(
            grad_qkv_local.reshape(width, 3 * inner) * proj_weight.astype(jnp.float32), axis=1
        )
        / norm_one
    )
    spread_one = grad_normed_one * norm_one
    grad_tokens = grad_hidden + inverse_one * (
        spread_one - scaled_one * jnp.mean(spread_one * scaled_one, axis=1, keepdims=True)
    )
    grad_qkv_sum, grad_out_sum, grad_bias_sum = lax.psum(
        (grad_qkv_local, grad_out_local, grad_bias_local), "dp"
    )
    small_sum = total_over_all(jnp.concatenate([grad_router, grad_norm_two[None]], axis=0))
    grad_router_sum = small_sum[:experts].T
    grad_two_sum = small_sum[experts]
    grad_one_sum = total_over_all(grad_norm_one[None])[0]
    return (
        mixed.astype(jnp.bfloat16),
        grad_tokens.astype(jnp.bfloat16),
        grad_one_sum,
        grad_qkv_sum,
        grad_out_sum,
        grad_bias_sum,
        grad_two_sum,
        grad_router_sum,
        grad_gate[None],
        grad_up[None],
        grad_down[None],
    )


def solution(mesh):
    return jax.shard_map(
        local,
        mesh=mesh,
        in_specs=(
            P(("dp", "tensor"), None),
            P("dp"),
            P(),
            P(("dp", "tensor"), None),
            P(),
            P(None, None, "tensor"),
            P("tensor", None),
            P(None, "tensor"),
            P(),
            P(),
            P("dp", None, "tensor"),
            P("dp", None, "tensor"),
            P("dp", "tensor", None),
            P(("dp", "tensor"), None),
        ),
        out_specs=(
            P(("dp", "tensor"), None),
            P(("dp", "tensor"), None),
            P(),
            P(None, None, "tensor"),
            P("tensor", None),
            P(None, "tensor"),
            P(),
            P(),
            P("dp", None, "tensor"),
            P("dp", None, "tensor"),
            P("dp", "tensor", None),
        ),
        check_vma=False,
    )
```

```python
import functools

import jax
import jax.numpy as jnp
from jax import lax
from jax.experimental import pallas as pl
from jax.experimental.pallas import tpu as pltpu
from jax.sharding import PartitionSpec as P

HD = 64


EPSILON = 1e-06
HIGHEST = lax.Precision.HIGHEST


def contract(left, right, left_dim, right_dim):
    return lax.dot_general(
        left, right, (((left_dim,), (right_dim,)), ((), ())), preferred_element_type=jnp.float32
    )


def gated(pre_gate, pre_up):
    return jax.nn.gelu(pre_gate, approximate=True) * pre_up


def exchange(rows):
    return lax.all_to_all(rows, "dp", split_axis=0, concat_axis=0, tiled=True)


def turned(table, first, width):
    return jnp.concatenate(
        [table[:, : first + 1][:, ::-1], table[:, first + 1 : width][:, ::-1]], axis=1
    )


def dot(left, right, left_dim, right_dim):
    return lax.dot_general(
        left, right, (((left_dim,), (right_dim,)), ((), ())), preferred_element_type=jnp.float32
    )


def block_probs(proj_ref, seg_col_ref, seg_row_ref, bias_ref, head, heads, first, block, scale):
    width = first + block
    inner = heads * HD
    rows = slice(first, width)
    query = proj_ref[rows, head * HD : (head + 1) * HD]
    key = proj_ref[:width, inner + head * HD : inner + (head + 1) * HD]
    base = jnp.broadcast_to(bias_ref[head, first // block, :width][None, :], (block, width))
    bias = pltpu.roll(base, 0, 1, stride=1, stride_axis=0)
    row = lax.broadcasted_iota(jnp.int32, (block, width), 0) + first
    column = lax.broadcasted_iota(jnp.int32, (block, width), 1)
    allowed = (column <= row) & (seg_col_ref[rows, :] == seg_row_ref[:, :width])
    scores = jnp.where(allowed, dot(query, key, 1, 1) * scale + bias, -1e30)
    weights = jnp.exp(scores - jnp.max(scores, axis=1, keepdims=True))
    return query, key, weights / jnp.sum(weights, axis=1, keepdims=True)


def attend_kernel(heads, block, scale, proj_ref, seg_col_ref, seg_row_ref, bias_ref, context_ref):
    length = proj_ref.shape[0]
    inner = heads * HD
    for first in range(0, length, block):
        width = first + block
        parts = []
        for head in range(heads):
            query, key, probs = block_probs(
                proj_ref, seg_col_ref, seg_row_ref, bias_ref, head, heads, first, block, scale
            )
            value = proj_ref[:width, 2 * inner + head * HD : 2 * inner + (head + 1) * HD]
            parts.append(dot(probs.astype(jnp.bfloat16), value, 1, 0))
        context_ref[first:width, :] = jnp.concatenate(parts, axis=1).astype(jnp.bfloat16)


def attend_back_kernel(
    heads,
    block,
    scale,
    proj_ref,
    grad_ref,
    seg_col_ref,
    seg_row_ref,
    bias_ref,
    rows_ref,
    diag_ref,
    total_ref,
):
    length = proj_ref.shape[0]
    inner = heads * HD
    total_ref[...] = jnp.zeros_like(total_ref)
    diag_ref[...] = jnp.zeros_like(diag_ref)
    flip = (
        lax.broadcasted_iota(jnp.int32, (block, block), 0)
        + lax.broadcasted_iota(jnp.int32, (block, block), 1)
        == block - 1
    ).astype(jnp.bfloat16)
    for first in range(0, length, block):
        width = first + block
        query_parts = []
        for head in range(heads):
            query, key, probs = block_probs(
                proj_ref, seg_col_ref, seg_row_ref, bias_ref, head, heads, first, block, scale
            )
            value = proj_ref[:width, 2 * inner + head * HD : 2 * inner + (head + 1) * HD]
            grad = grad_ref[first:width, head * HD : (head + 1) * HD]
            grad_probs = dot(grad, value, 1, 1)
            row_delta = jnp.sum(probs * grad_probs, axis=1, keepdims=True)
            grad_scores = (probs * (grad_probs - row_delta)).astype(jnp.bfloat16)
            query_parts.append(dot(grad_scores, key, 1, 0) * scale)
            total_ref[0, head, :width, :] += dot(grad_scores, query, 0, 0) * scale
            total_ref[1, head, :width, :] += dot(probs.astype(jnp.bfloat16), grad, 0, 0)
            flipped = dot(flip, grad_scores, 1, 0)
            lined = pltpu.roll(flipped, 0, 1, stride=1, stride_axis=0)
            diag_ref[head, first // block, :width] = jnp.sum(lined, axis=0)
        rows_ref[first:width, :inner] = jnp.concatenate(query_parts, axis=1).astype(jnp.bfloat16)
    for part in range(2):
        rows_ref[:, (1 + part) * inner : (2 + part) * inner] = jnp.concatenate(
            [total_ref[part, head] for head in range(heads)], axis=1
        ).astype(jnp.bfloat16)


def local(
    tokens,
    segments,
    buckets,
    routes,
    norm_one,
    w_qkv,
    w_out,
    rel_bias,
    norm_two,
    w_router,
    w_gate,
    w_up,
    w_down,
    cotangent,
):
    rows_dev = tokens.shape[0]
    width = tokens.shape[1]
    tok_dev = segments.shape[0]
    bucket_count = rel_bias.shape[0]
    heads_local = rel_bias.shape[1]
    inner = heads_local * HD
    experts = w_router.shape[1]
    groups = lax.axis_size("tensor")
    dp_count = lax.axis_size("dp")
    capacity = 4 * tok_dev // (groups * experts)
    top = routes.shape[1]
    block = min(256, tok_dev)
    blocks = tok_dev // block
    scale = HD ** (-0.5)
    upstream = cotangent.astype(jnp.float32)
    values = tokens.astype(jnp.float32)
    inverse_one = lax.rsqrt(jnp.mean(values * values, axis=1, keepdims=True) + EPSILON)
    scaled_one = values * inverse_one
    normed_one = (scaled_one * norm_one).astype(jnp.bfloat16)
    side_all = lax.all_gather(
        jnp.concatenate(
            [
                normed_one,
                cotangent,
                jnp.pad(routes.astype(jnp.bfloat16), ((0, 0), (0, 128 - top))),
            ],
            axis=1,
        ),
        "tensor",
        axis=0,
        tiled=True,
    )
    normed_all = side_all[:, :width]
    side_all = side_all[:, width:]
    cotangent_all = side_all[:, :width].reshape(groups, rows_dev, width)
    routes_all = side_all[:, width : width + top].astype(jnp.int32).reshape(groups, rows_dev, top)
    choose = (routes_all[..., None] == jnp.arange(experts, dtype=jnp.int32)).astype(jnp.float32)
    member = jnp.sum(choose, axis=2)
    earlier = jnp.tril(jnp.ones((rows_dev, rows_dev), jnp.bfloat16), -1)
    place = jnp.einsum(
        "nm,tme->tne", earlier, member.astype(jnp.bfloat16), preferred_element_type=jnp.float32
    )
    seat = place + capacity * jnp.arange(experts, dtype=jnp.float32)
    slot = jnp.sum(choose * seat[:, :, None, :], axis=3).astype(jnp.int32)
    seats = jnp.arange(experts * capacity, dtype=jnp.int32)
    pick = [slot[:, :, k, None] == seats for k in range(top)]
    pick_any = pick[0]
    for one in pick[1:]:
        pick_any = pick_any | one
    pick_any = pick_any.astype(jnp.bfloat16)

    def send(group_rows):
        seated = jnp.einsum(
            "tnz,tnd->tzd", pick_any, group_rows, preferred_element_type=jnp.float32
        ).astype(jnp.bfloat16)
        ordered = seated.reshape(groups, experts, capacity, width).transpose(1, 0, 2, 3)
        return exchange(ordered.reshape(experts, groups * capacity, width)).reshape(-1, width)

    def fetch_raw(rows_back):
        return exchange(rows_back.reshape(dp_count, groups * capacity, width))

    def gather_back(returned):
        ordered = returned.reshape(experts, groups, capacity, width).transpose(1, 0, 2, 3)
        summed = jnp.einsum(
            "tnz,tzd->tnd",
            pick_any,
            ordered.reshape(groups, experts * capacity, width),
            preferred_element_type=jnp.float32,
        )
        return lax.psum_scatter(
            summed.astype(jnp.bfloat16).reshape(tok_dev, width),
            "tensor",
            scatter_dimension=0,
            tiled=True,
        ).astype(jnp.float32)

    cot_rows = send(cotangent_all)
    proj_weight = w_qkv.reshape(width, 3 * inner)
    projected = jnp.dot(normed_all, proj_weight, preferred_element_type=jnp.float32).astype(
        jnp.bfloat16
    )
    bucket_hot = (buckets[:, None] == jnp.arange(bucket_count, dtype=jnp.int32)[None, :]).astype(
        jnp.float32
    )
    bias_dist = jnp.dot(bucket_hot, rel_bias, precision=HIGHEST).T
    bias_table = jnp.stack(
        [
            jnp.pad(
                turned(bias_dist, first, first + block), ((0, 0), (0, tok_dev - first - block))
            )
            for first in range(0, tok_dev, block)
        ],
        axis=1,
    )
    seg_col = segments[:, None]
    seg_row = segments[None, :]
    flops = 2 * heads_local * tok_dev * tok_dev * HD
    context = pl.pallas_call(
        functools.partial(attend_kernel, heads_local, block, scale),
        out_shape=jax.ShapeDtypeStruct((tok_dev, inner), jnp.bfloat16),
        cost_estimate=pl.CostEstimate(
            flops=2 * flops, bytes_accessed=2 * tok_dev * inner * 4, transcendentals=flops // 128
        ),
    )(projected, seg_col, seg_row, bias_table)
    rows = context
    attended = lax.psum_scatter(
        jnp.dot(rows, w_out, preferred_element_type=jnp.float32).astype(jnp.bfloat16),
        "tensor",
        scatter_dimension=0,
        tiled=True,
    ).astype(jnp.float32)
    hidden = values + attended
    inverse_two = lax.rsqrt(jnp.mean(hidden * hidden, axis=1, keepdims=True) + EPSILON)
    scaled_two = hidden * inverse_two
    normed_two = (scaled_two * norm_two).astype(jnp.bfloat16)
    normed_two_all = lax.all_gather(normed_two, "tensor", axis=0, tiled=True)
    normed_two_all, cot_rows = lax.optimization_barrier((normed_two_all, cot_rows))
    rows_in = send(normed_two_all.reshape(groups, rows_dev, width))
    own_expert = (jnp.arange(experts, dtype=jnp.int32) == lax.axis_index("dp")).astype(jnp.float32)
    router_rows = jax.nn.softmax(
        jnp.dot(rows_in, w_router, preferred_element_type=jnp.float32), axis=1
    )
    gate_rows = jnp.sum(own_expert * router_rows, axis=1, keepdims=True)
    grad_in = (gate_rows * cot_rows.astype(jnp.float32)).astype(jnp.bfloat16)
    gate_weight = w_gate[0]
    up_weight = w_up[0]
    down_weight = w_down[0]
    pre_gate = jnp.dot(rows_in, gate_weight, preferred_element_type=jnp.float32)
    pre_up = jnp.dot(rows_in, up_weight, preferred_element_type=jnp.float32)
    active = gated(pre_gate, pre_up).astype(jnp.bfloat16)
    partial_rows = jnp.dot(active, down_weight, preferred_element_type=jnp.float32)
    grad_gates = jnp.sum(partial_rows * cot_rows.astype(jnp.float32), axis=1, keepdims=True)
    mix_rows = (gate_rows * partial_rows).astype(jnp.bfloat16)
    grad_logits = (grad_gates * gate_rows * (own_expert - router_rows)).astype(jnp.bfloat16)
    grad_router = contract(grad_logits, rows_in, 0, 0)
    grad_active = contract(grad_in, down_weight, 1, 1)
    grad_down = contract(active, grad_in, 0, 0)
    unused, pull = jax.vjp(gated, pre_gate, pre_up)
    grad_pre_gate, grad_pre_up = pull(grad_active)
    grad_pre_gate = grad_pre_gate.astype(jnp.bfloat16)
    grad_pre_up = grad_pre_up.astype(jnp.bfloat16)
    grad_gate = contract(rows_in, grad_pre_gate, 0, 0)
    grad_up = contract(rows_in, grad_pre_up, 0, 0)
    grad_rows_x = (
        contract(grad_pre_gate, gate_weight, 1, 1)
        + contract(grad_pre_up, up_weight, 1, 1)
        + contract(grad_logits, w_router, 1, 1)
    ).astype(jnp.bfloat16)
    grad_back, grad_gate, grad_up, grad_down, mix_rows, grad_router = lax.optimization_barrier(
        (fetch_raw(grad_rows_x), grad_gate, grad_up, grad_down, mix_rows, grad_router)
    )
    mixing = gather_back(fetch_raw(mix_rows))
    grad_normed_two = gather_back(grad_back)
    mixed = hidden + mixing
    grad_norm_two = jnp.sum(grad_normed_two * scaled_two, axis=0)
    spread_two = grad_normed_two * norm_two
    grad_hidden = upstream + inverse_two * (
        spread_two - scaled_two * jnp.mean(spread_two * scaled_two, axis=1, keepdims=True)
    )
    grad_attended = grad_hidden.astype(jnp.bfloat16)
    piece = lax.all_gather(grad_attended, "tensor", axis=0, tiled=True)
    rows = context
    grad_out_sum = contract(rows, piece, 0, 0)
    grad_piece = contract(piece, w_out, 1, 1)
    grad_context_all = grad_piece
    grad_out_local, grad_context_all = (grad_out_sum, grad_context_all)
    grad_context = grad_context_all.astype(jnp.bfloat16)
    grad_proj_rows, diagonals = pl.pallas_call(
        functools.partial(attend_back_kernel, heads_local, block, scale),
        out_shape=(
            jax.ShapeDtypeStruct((tok_dev, 3 * inner), jnp.bfloat16),
            jax.ShapeDtypeStruct((heads_local, blocks, tok_dev), jnp.float32),
        ),
        scratch_shapes=[pltpu.VMEM((2, heads_local, tok_dev, HD), jnp.float32)],
        cost_estimate=pl.CostEstimate(
            flops=5 * flops, bytes_accessed=4 * tok_dev * inner * 4, transcendentals=flops // 128
        ),
    )(projected, grad_context, seg_col, seg_row, bias_table)
    by_distance = jnp.zeros((heads_local, tok_dev), jnp.float32)
    for index in range(blocks):
        first = index * block
        reach = first + block
        sums = jnp.roll(diagonals[:, index, :reach], 1 - block, axis=1)
        by_distance = by_distance + jnp.pad(
            turned(sums, first, reach), ((0, 0), (0, tok_dev - reach))
        )
    grad_bias_local = jnp.einsum("hn,nb->bh", by_distance, bucket_hot, precision=HIGHEST)
    grad_qkv_local = contract(normed_all, grad_proj_rows, 0, 0).reshape(width, 3, inner)
    rows = grad_proj_rows
    grad_normed_one = lax.psum_scatter(
        contract(rows, proj_weight, 1, 1).astype(jnp.bfloat16),
        "tensor",
        scatter_dimension=0,
        tiled=True,
    ).astype(jnp.float32)
    grad_norm_one = (
        jnp.sum(
            grad_qkv_local.reshape(width, 3 * inner) * proj_weight.astype(jnp.float32), axis=1
        )
        / norm_one
    )
    spread_one = grad_normed_one * norm_one
    grad_tokens = grad_hidden + inverse_one * (
        spread_one - scaled_one * jnp.mean(spread_one * scaled_one, axis=1, keepdims=True)
    )
    small = jnp.concatenate(
        [
            grad_router,
            grad_norm_two[None],
            grad_norm_one[None],
            jnp.pad(
                grad_bias_local.reshape(1, -1),
                ((0, 0), (0, width - bucket_count * heads_local)),
            ),
        ],
        axis=0,
    )
    grad_qkv_sum, grad_out_sum, small = lax.psum((grad_qkv_local, grad_out_local, small), "dp")
    grad_bias_sum = small[experts + 2, : bucket_count * heads_local].reshape(
        bucket_count, heads_local
    )
    total = lax.psum(small[: experts + 2], "tensor")
    grad_router_sum = total[:experts].T
    grad_two_sum = total[experts]
    grad_one_sum = total[experts + 1]
    return (
        mixed.astype(jnp.bfloat16),
        grad_tokens.astype(jnp.bfloat16),
        grad_one_sum,
        grad_qkv_sum,
        grad_out_sum,
        grad_bias_sum,
        grad_two_sum,
        grad_router_sum,
        grad_gate[None],
        grad_up[None],
        grad_down[None],
    )


def solution(mesh):
    return jax.shard_map(
        local,
        mesh=mesh,
        in_specs=(
            P(("dp", "tensor"), None),
            P("dp"),
            P(),
            P(("dp", "tensor"), None),
            P(),
            P(None, None, "tensor"),
            P("tensor", None),
            P(None, "tensor"),
            P(),
            P(),
            P("dp", None, "tensor"),
            P("dp", None, "tensor"),
            P("dp", "tensor", None),
            P(("dp", "tensor"), None),
        ),
        out_specs=(
            P(("dp", "tensor"), None),
            P(("dp", "tensor"), None),
            P(),
            P(None, None, "tensor"),
            P("tensor", None),
            P(None, "tensor"),
            P(),
            P(),
            P("dp", None, "tensor"),
            P("dp", None, "tensor"),
            P("dp", "tensor", None),
        ),
        check_vma=False,
    )
```
